128 devices in a mesh: grp: 2 (over core), row: 8 (over z, y_lo), col: 8 (over x, y_hi).
Axes of the slice: x: 4, y: 4 (y_hi: 2, y_lo: 2; y = y_hi * 2 + y_lo), z: 4, core: 2. Of those that a mesh axis runs over, the one named last changes fastest.
Arguments:
- cost_matrix: float32 [2, 8192, 8192], P('grp', 'row', 'col'), may hold values from -0.09375 to 0.09375
- coupling_factors: float32 [2, 8192, 1024], P('grp', ('row', 'col')), may hold values from 0.25 to 4
Outputs:
- updated_factors: float32 [2, 8192, 1024], P('grp', ('row', 'col'))
The draws below stay inside these ranges and needn't reach their ends.
All inputs are finite; a program needn't handle non-finite values. Where the reference program divides by a largest or mean magnitude, that divisor is 1e-20 or more.
Results may differ from the reference program's by a relative error of at most 0.0003.
Values sent between devices are 32-bit elements; how exact they have to be, the bound alone decides.
No kernel may reach another device: no remote copies, remote signals or barrier semaphores. Data moves between devices by JAX's collectives and lax.ppermute only.
A program may use at most 64 MiB of HBM per device.

```python
import math
import jax
import jax.numpy as jnp
from jax import lax

RANK = 1024
STEPS = 2
N = 8192


def with_spikes(values, stream_key, source, target, parts, factor):
    owner, partner = [(jnp.arange(values.shape[axis_at]) // (values.shape[axis_at] // parts)).reshape([-1 if axis == axis_at else 1 for axis in range(values.ndim)]) for axis_at in (source, target)]
    chosen = jax.random.permutation(stream_key, parts)[partner]
    strong = (owner == chosen) | (owner == (partner + parts // 2) % parts)
    return jnp.where(strong, factor * values, values)


def shard_levels(stream_key, dims, pieces, least, top_value):
    loudness = 1.0
    for position, shards_of in pieces:
        draws = jax.random.uniform(jax.random.fold_in(jax.random.fold_in(stream_key, 6), position), (shards_of,), jnp.float32, least / len(pieces), top_value / len(pieces))
        loudness = loudness * jnp.repeat(jnp.exp(draws), dims[position] // shards_of).reshape((-1,) + (1,) * (len(dims) - 1 - position))
    return loudness


def gaussian_with(stream_key, extent, deviation, limit, split, heavy, kind=jnp.bfloat16):
    result = deviation * jax.random.normal(stream_key, extent, jnp.float32)
    if split:
        result = result * shard_levels(stream_key, extent, split, -0.22, 0.18)
    return jnp.clip(with_spikes(result, jax.random.fold_in(stream_key, 3), *heavy), -limit, limit).astype(kind)


def setup_inputs(seed: int = 0) -> dict:
    streams_of = jax.random.split(jax.random.key(seed), 3)
    cost_matrix = gaussian_with(streams_of[0], (2, N, N), N ** -0.5, 0.09375, ((0, 2), (1, 8), (2, 8)), (2, 1, 8, 2.0), jnp.float32)
    coupling_factors = jnp.clip(jnp.exp(math.log(4.0) - 2.7725887 * jax.random.uniform(streams_of[1], (2, N, RANK), jnp.float32) ** shard_levels(streams_of[1], (2, N, RANK), ((0, 2), (1, 64)), -0.2, 0.2)), 0.25, 4.0)
    return {"cost_matrix": cost_matrix, "coupling_factors": coupling_factors}


def reference(cost_matrix, coupling_factors):
    rank_width = coupling_factors.shape[2]
    factor_list = [coupling_factors[0], coupling_factors[1]]
    for iteration in range(STEPS):
        mixed = [jnp.dot(cost_matrix[group_id], factor_list[group_id], precision=lax.Precision.HIGHEST, preferred_element_type=jnp.float32) for group_id in range(2)]
        cores = [jnp.dot(factor_list[group_id].T, mixed[group_id], precision=lax.Precision.HIGHEST, preferred_element_type=jnp.float32) for group_id in range(2)]
        updated = []
        for group_id in range(2):
            gradient = jnp.dot(mixed[group_id], cores[1 - group_id], precision=lax.Precision.HIGHEST, preferred_element_type=jnp.float32)
            row_scale = jnp.max(jnp.abs(gradient), axis=1, keepdims=True) + 1e-6
            exponent = -3.0 * gradient / row_scale
            weighted = factor_list[group_id] * jnp.exp(exponent)
            updated.append(rank_width * weighted / jnp.sum(weighted, axis=1, keepdims=True))
        factor_list = updated
    return jnp.stack(factor_list)
```

```python
import jax
import jax.numpy as jnp
from jax import lax
from jax.sharding import PartitionSpec as P

STEPS = 2
HIGH = lax.Precision.HIGH


def exchange(pieces, axes):
    return lax.all_to_all(pieces, axes, split_axis=0, concat_axis=0, tiled=True)


def dot(a, b, contract):
    return lax.dot_general(
        a, b, (contract, ((), ())), precision=HIGH, preferred_element_type=jnp.float32
    )


def shards(cost_matrix, coupling_factors):
    cost_tile = cost_matrix[0]
    current = coupling_factors[0]
    rows_side = lax.axis_size("row")
    cols_side = lax.axis_size("col")
    everyone = rows_side * cols_side
    blk_rows = cost_tile.shape[0]
    piece_rows, rank_width = current.shape
    sub_rows = piece_rows // rows_side
    core_rows = rank_width // everyone
    swap = [(i, i ^ 1) for i in range(lax.axis_size("grp"))]
    current = exchange(current, "row")
    for iteration in range(STEPS):
        pieces = current.reshape(cols_side, 1, sub_rows, rank_width)
        sent = jnp.broadcast_to(pieces, (cols_side, rows_side, sub_rows, rank_width))
        panel_rows = exchange(
            sent.reshape(everyone * sub_rows, rank_width), ("col", "row")
        )
        partial = dot(cost_tile, panel_rows, ((1,), (0,)))
        parts = exchange(partial, ("col", "row"))
        mixed = parts.reshape(cols_side, piece_rows, rank_width).sum(0)
        core_part = dot(current, mixed, ((0,), (0,)))
        core_rows_parts = exchange(core_part, ("row", "col"))
        core_piece = core_rows_parts.reshape(everyone, core_rows, rank_width).sum(0)
        other_piece = lax.ppermute(core_piece, "grp", swap)
        other_core = exchange(
            jnp.broadcast_to(other_piece[None], (everyone, core_rows, rank_width)).reshape(
                rank_width, rank_width
            ),
            ("row", "col"),
        )
        gradient = dot(mixed, other_core, ((1,), (0,)))
        row_scale = jnp.max(jnp.abs(gradient), axis=1, keepdims=True) + 1e-06
        exponent = -3.0 * gradient / row_scale
        weighted = current * jnp.exp(exponent)
        current = rank_width * weighted / jnp.sum(weighted, axis=1, keepdims=True)
    return exchange(current, "row")[None]


def solution(mesh):
    in_specs = (P("grp", "row", "col"), P("grp", ("row", "col"), None))
    out_specs = P("grp", ("row", "col"), None)
    return jax.shard_map(shards, mesh=mesh, in_specs=in_specs, out_specs=out_specs, check_vma=False)
```

```python
import jax
import jax.numpy as jnp
from jax import lax
from jax.sharding import Mesh
from jax.sharding import PartitionSpec as P

STEPS = 2
HIGH = lax.Precision.HIGH
SIZES = {"grp": 2, "z": 4, "yl": 2, "x": 4, "yh": 2}
PLANE = ("x", "yh", "yl")


def exchange(pieces, axes):
    return lax.all_to_all(pieces, axes, split_axis=0, concat_axis=0, tiled=True)


def spread(piece, axes, count):
    return exchange(jnp.broadcast_to(piece[None], (count,) + piece.shape), axes)


def dot(a, b, contract):
    return lax.dot_general(
        a, b, (contract, ((), ())), precision=HIGH, preferred_element_type=jnp.float32
    )


def shards(cost_matrix, coupling_factors):
    nz, nyl, nx, nyh = (SIZES[a] for a in ("z", "yl", "x", "yh"))
    blocks, plane = nz * nyl, nx * nyh * nyl
    cost_tile = cost_matrix[0]
    start = coupling_factors[0]
    blk_rows = cost_tile.shape[0]
    piece_rows, rank = start.shape
    sub, wide = piece_rows // nyl, rank // nz
    rows = blocks * sub
    swap = [(0, 1), (1, 0)]
    start = start.reshape(nyl, sub, nz, wide).transpose(2, 0, 1, 3)
    current = exchange(start.reshape(blocks, sub, wide), ("z", "yl"))
    for iteration in range(STEPS):
        flat = current.reshape(rows, wide)
        whole = spread(flat, "z", nz)
        sent = jnp.broadcast_to(current[:, None], (blocks, nyl, sub, wide))
        panel = exchange(sent.reshape(plane, sub, wide), PLANE).reshape(blk_rows, wide)
        panels = spread(panel, "z", nz)
        partial = jnp.einsum(
            "mk,zkn->mzn", cost_tile, panels, precision=HIGH, preferred_element_type=jnp.float32
        ).reshape(nx, blk_rows // nx, rank)
        half = exchange(partial, "x").sum(0)
        half = half.reshape(nyh, nyl, sub, nz, wide).transpose(0, 3, 1, 2, 4)
        mixed = exchange(half.reshape(nyh * blocks, sub, wide), ("yh", "z", "yl"))
        mixed = mixed.reshape(nyh, rows, wide).sum(0)
        mixed_whole = spread(mixed, "z", nz)
        core_part = jnp.einsum(
            "zra,rn->zan", whole, mixed, precision=HIGH, preferred_element_type=jnp.float32
        )
        core = exchange(core_part.reshape(plane, rank // plane, wide), PLANE).sum(0)
        core = lax.ppermute(core, "grp", swap)
        core = spread(core, PLANE, plane).reshape(nz, wide, wide)
        gradient = jnp.einsum(
            "zra,zan->rn", mixed_whole, core, precision=HIGH, preferred_element_type=jnp.float32
        )
        top = spread(jnp.max(jnp.abs(gradient), axis=1), "z", nz).max(0)
        row_scale = top[:, None] + 1e-06
        weighted = flat * jnp.exp(-3.0 * gradient / row_scale)
        total = spread(jnp.sum(weighted, axis=1), "z", nz).sum(0)
        current = (rank * weighted / total[:, None]).reshape(blocks, sub, wide)
    out = exchange(current, ("z", "yl")).reshape(nz, nyl, sub, wide)
    return out.transpose(1, 2, 0, 3).reshape(1, piece_rows, rank)


def solution(mesh):
    fine = Mesh(mesh.devices.reshape(tuple(SIZES.values())), tuple(SIZES))
    in_specs = (P("grp", ("z", "yl"), ("x", "yh")), P("grp", ("z", "yl", "x", "yh"), None))
    out_specs = P("grp", ("z", "yl", "x", "yh"), None)
    return jax.shard_map(shards, mesh=fine, in_specs=in_specs, out_specs=out_specs, check_vma=False)
```

```python
import jax
import jax.numpy as jnp
from jax import lax
from jax.sharding import Mesh
from jax.sharding import PartitionSpec as P

STEPS = 2
HIGH = lax.Precision.HIGH
SIZES = {"grp": 2, "z": 4, "yl": 2, "x": 4, "yh": 2}
SIDE = ("z", "yl", "x", "yh")
PLANE = ("x", "yh", "yl")


def place(z, yl, x, yh):
    return ((z % 4 * 2 + yl) * 4 + x % 4) * 2 + yh


ROW_CODES = [
    [place(q + 2 * m, m, x, yh) for m in range(2) for x in range(4) for yh in range(2)]
    for q in range(4)
]
COL_CODES = [
    [place(z, yl, q + 2 * m, m) for m in range(2) for z in range(4) for yl in range(2)]
    for q in range(4)
]


def exchange(pieces, axes, groups=None):
    return lax.all_to_all(
        pieces, axes, split_axis=0, concat_axis=0, tiled=True, axis_index_groups=groups
    )


def spread(piece, axes, count):
    return exchange(jnp.broadcast_to(piece[None], (count,) + piece.shape), axes)


def shift(value, axis, by):
    size = SIZES[axis]
    return lax.ppermute(value, axis, [(i, (i + by) % size) for i in range(size)])


def from_ring(value):
    return [value] + [shift(value, "z", -d) for d in (1, 2, 3)]


def dot(a, b, contract):
    return lax.dot_general(
        a, b, (contract, ((), ())), precision=HIGH, preferred_element_type=jnp.float32
    )


def shards(cost_matrix, coupling_factors):
    nz, nyl, nx, nyh = (SIZES[a] for a in SIDE)
    blocks, plane = nz * nyl, nx * nyh * nyl
    cost_tile = cost_matrix[0]
    start = coupling_factors[0]
    blk_rows = cost_tile.shape[0]
    piece_rows, rank = start.shape
    sub, wide = piece_rows // nyl, rank // nz
    rows = blocks * sub
    row_code = (lax.axis_index("z") + 2 * lax.axis_index("yl")) & 3
    col_code = (lax.axis_index("x") + 2 * lax.axis_index("yh")) & 3
    tiles = []
    for d in range(4):
        found = [
            lax.dynamic_slice_in_dim(
                cost_tile, ((col_code + d + 2 * m & 3) * 2 + m) * piece_rows, piece_rows
            )
            for m in range(2)
        ]
        tiles.append(jnp.concatenate(found))
    start = start.reshape(nyl, sub, nz, wide).transpose(2, 0, 1, 3)
    current = exchange(start.reshape(blocks, sub, wide), ("z", "yl"))

    def step(_, current):
        flat = current.reshape(rows, wide)
        own = exchange(jnp.concatenate([current, current]), SIDE, ROW_CODES)
        own = own.reshape(2, blocks, sub, wide)
        near = [own, shift(own, "z", -1), shift(own, "yl", 1), shift(own, "z", 1)]
        panel = jnp.concatenate(
            [
                jnp.stack([near[e][0], near[(e + 2) % 4][1]], axis=1).reshape(blk_rows, wide)
                for e in range(4)
            ],
            axis=1,
        )
        parts = [dot(tiles[d], panel, ((1,), (0,))) for d in range(4)]
        ready, parts[1] = lax.optimization_barrier((flat, parts[1]))
        whole = from_ring(ready)
        half = (
            (parts[0] + shift(parts[1], "x", 1)) + shift(parts[3], "x", -1)
        ) + shift(parts[2], "yh", 1)
        half, whole = lax.optimization_barrier((half, whole))
        half = half.reshape(nyh, nyl, sub, nz, wide).transpose(0, 3, 1, 2, 4)
        half = jnp.roll(half, row_code, axis=1)
        mixed = exchange(half.reshape(nyh * blocks, sub, wide), SIDE, COL_CODES)
        mixed = mixed.reshape(nyh, rows, wide).sum(0)
        mixed_whole = from_ring(mixed)
        core_part = dot(jnp.concatenate(whole, axis=1), mixed, ((0,), (0,)))
        core = exchange(core_part.reshape(plane, rank // plane, wide), PLANE).sum(0)
        core, mixed_whole = lax.optimization_barrier((core, mixed_whole))
        core = shift(core, "grp", 1)
        core = spread(core, PLANE, plane)
        gradient = dot(
            jnp.concatenate(mixed_whole, axis=1), core.reshape(rank, wide), ((1,), (0,))
        )
        top = jnp.max(spread(jnp.max(jnp.abs(gradient), axis=1), "z", nz), axis=0)
        row_scale = top[:, None] + 1e-06
        weighted = flat * jnp.exp(-3.0 * gradient / row_scale)
        total = jnp.sum(spread(jnp.sum(weighted, axis=1), "z", nz), axis=0)
        return (rank * weighted / total[:, None]).reshape(blocks, sub, wide)

    current = lax.fori_loop(0, STEPS, step, current)
    out = exchange(current, ("z", "yl")).reshape(nz, nyl, sub, wide)
    return out.transpose(1, 2, 0, 3).reshape(1, piece_rows, rank)


def solution(mesh):
    fine = Mesh(mesh.devices.reshape(tuple(SIZES.values())), tuple(SIZES))
    in_specs = (P("grp", ("z", "yl"), ("x", "yh")), P("grp", SIDE, None))
    return jax.shard_map(
        shards, mesh=fine, in_specs=in_specs, out_specs=P("grp", SIDE, None), check_vma=False
    )
```
